32 devices in a mesh: fibre: 4 (over z), cols: 8 (over y, x, core).
Axes of the slice: x: 2, y: 2, z: 4, core: 2. Of those that a mesh axis runs over, the one named last changes fastest.
Arguments:
- tensor: float32 [512, 8, 4, 2048], P('fibre', 'cols'), may hold values from -6 to 6
- initial: float32 [512, 64], replicated, may hold values from -6 to 6
Outputs:
- core_slab: float32 [64, 8, 4, 2048], P(None, 'cols', 'fibre')
- basis: float32 [512, 64], replicated
The draws below stay inside these ranges and needn't reach their ends.
All inputs are finite; a program needn't handle non-finite values.
Results may differ from the reference program's by a relative error of at most 0.0002.
Values sent between devices are 32-bit elements; how exact they have to be, the bound alone decides.
No kernel may reach another device: no remote copies, remote signals or barrier semaphores. Data moves between devices by JAX's collectives and lax.ppermute only.
A program may use at most 64 MiB of HBM per device.

```python
import jax
import jax.numpy as jnp
from jax import lax

M = 512
RANK = 64
COLS_DEV = 2048
ITERS = 2
N_FIBRE = 4
N_COLS = 8


def level_of(key, extent, split, least, top_value):
    level, own = 1.0, jax.random.fold_in(key, 6)
    for position, blocks in split:
        draws = jnp.exp(jax.random.uniform(jax.random.fold_in(own, position), (blocks,), jnp.float32, least / len(split), top_value / len(split)))
        level = level * jnp.repeat(draws, extent[position] // blocks).reshape([-1 if axis == position else 1 for axis in range(len(extent))])
    return level


def centred(rng, dims, deviation, most, pieces=(), held_as=jnp.bfloat16):
    drawn = jax.random.normal(rng, dims, jnp.float32) * deviation
    if len(pieces) > 0:
        drawn = level_of(rng, dims, pieces, -0.22, 0.18) * drawn
    return jnp.clip(drawn, min=-most, max=most).astype(held_as)


def setup_inputs(seed: int = 0) -> dict:
    seeds = jax.random.split(jax.random.key(seed), 3)
    tensor = centred(seeds[0], (M, N_COLS, N_FIBRE, COLS_DEV), 1.0, 6.0, ((0, 4), (1, 8)), jnp.float32)
    initial = centred(seeds[1], (M, RANK), 1.0, 6.0, (), jnp.float32)
    return dict(tensor=tensor, initial=initial)


def orthonormal(product):
    squares = jnp.dot(product.T, product, precision=lax.Precision.HIGHEST)
    lower = jnp.linalg.cholesky(squares)
    return lax.linalg.triangular_solve(lower, product, left_side=False, lower=True, transpose_a=True)

def reference(tensor, initial):
    modes = tensor.shape[0]
    matrix = tensor.reshape(modes, -1)
    gram = jnp.dot(matrix, matrix.T, precision=lax.Precision.HIGHEST)
    basis = initial
    for step in range(ITERS):
        basis = orthonormal(jnp.dot(gram, basis, precision=lax.Precision.HIGHEST))
    core_slab = jnp.dot(basis.T, matrix, precision=lax.Precision.HIGHEST)
    core_slab = core_slab.reshape(RANK, N_COLS, N_FIBRE, COLS_DEV)
    return (core_slab, basis)
```

```python
import jax
import jax.numpy as jnp
from jax import lax
from jax.sharding import PartitionSpec as P

ITERS = 2
HIGHEST = lax.Precision.HIGHEST


def dot(a, b, dims):
    return lax.dot_general(
        a, b, (dims, ((), ())), precision=HIGHEST, preferred_element_type=jnp.float32
    )


def swap(value, axis, size, bit):
    return lax.ppermute(value, axis, [(i, i ^ bit) for i in range(size)])


def bits(size):
    return [1 << b for b in range(size.bit_length() - 1)]


def block_order(value, blocks, bit):
    width = value.shape[1] // blocks
    parts = [value[:, k * width : (k + 1) * width] for k in range(blocks)]
    return jnp.concatenate([parts[k ^ bit] for k in range(blocks)], axis=1)


def total(value, n_fibre, n_cols):
    half = value.shape[0] // 2
    core = lax.axis_index("cols") % 2
    mine = lax.dynamic_slice_in_dim(value, core * half, half, 0)
    other = lax.dynamic_slice_in_dim(value, (1 - core) * half, half, 0)
    mine = mine + swap(other, "cols", n_cols, 1)
    for bit in bits(n_cols)[1:]:
        mine = mine + swap(mine, "cols", n_cols, bit)
    for bit in bits(n_fibre):
        mine = mine + block_order(swap(mine, "fibre", n_fibre, bit), n_fibre, bit)
    other = swap(mine, "cols", n_cols, 1)
    low = jnp.where(core == 0, mine, other)
    high = jnp.where(core == 0, other, mine)
    return jnp.concatenate([low, high], axis=0)


def inverse_factor(squares):
    lower = jnp.linalg.cholesky(squares)
    eye = jnp.eye(squares.shape[0], dtype=squares.dtype)
    return lax.linalg.triangular_solve(lower, eye, left_side=True, lower=True)


def shards(n_fibre, n_cols, tensor, initial):
    rows, width = tensor.shape[0], tensor.shape[3]
    me = lax.axis_index("fibre")

    def piece(k):
        return lax.dynamic_index_in_dim(tensor, me ^ k, 2, keepdims=False)[:, 0, :]

    order = list(range(n_fibre - 1, 0, -1))
    pieces = {k: swap(piece(k), "fibre", n_fibre, k) for k in order}
    pieces[0] = piece(0)
    columns = jnp.concatenate([pieces[k] for k in range(n_fibre)], axis=0)
    start = jnp.concatenate(
        [lax.dynamic_slice_in_dim(initial, (me ^ k) * rows, rows, 0) for k in range(n_fibre)], axis=0
    )

    def product(basis_t):
        inner = dot(basis_t, columns, ((1,), (0,)))
        return dot(inner, columns, ((1,), (1,)))

    basis_t = start.T
    inverse = None
    for step in range(ITERS):
        image = total(product(basis_t), n_fibre, n_cols)
        if inverse is not None:
            image = dot(inverse, image, ((1,), (0,)))
        inverse = inverse_factor(dot(image, image, ((1,), (1,))))
        basis_t = image
    basis_t = dot(inverse, basis_t, ((1,), (0,)))
    ranks = basis_t.shape[0]
    core_slab = dot(basis_t, columns, ((1,), (0,))).reshape(ranks, 1, 1, width)
    basis = basis_t.T
    basis = jnp.concatenate(
        [lax.dynamic_slice_in_dim(basis, (me ^ k) * rows, rows, 0) for k in range(n_fibre)], axis=0
    )
    return (core_slab, basis)


def solution(mesh):
    n_fibre, n_cols = mesh.shape["fibre"], mesh.shape["cols"]
    placed = (P("fibre", "cols", None, None), P())
    return jax.shard_map(
        lambda tensor, initial: shards(n_fibre, n_cols, tensor, initial),
        mesh=mesh,
        in_specs=placed,
        out_specs=(P(None, "cols", "fibre", None), P()),
        check_vma=False,
    )
```

```python
import functools

import jax
import jax.numpy as jnp
from jax import lax
from jax.experimental import pallas as pl
from jax.experimental.pallas import tpu as pltpu
from jax.sharding import PartitionSpec as P

ITERS = 2
HIGHEST = lax.Precision.HIGHEST
VMEM = pl.BlockSpec(memory_space=pltpu.VMEM)
ANY = pl.BlockSpec(memory_space=pl.ANY)
SMEM = pl.BlockSpec(memory_space=pltpu.SMEM)
ELIMINATE = 8
PROJECT = 512


def params(mib):
    return pltpu.CompilerParams(vmem_limit_bytes=mib << 20)


def f32(*shape):
    return jax.ShapeDtypeStruct(shape, jnp.float32)


def bf16(*shape):
    return jax.ShapeDtypeStruct(shape, jnp.bfloat16)


def dot(a, b, contract, precision=None):
    return lax.dot_general(
        a, b, (contract, ((), ())), precision=precision, preferred_element_type=jnp.float32
    )


NN = ((1,), (0,))
NT = ((1,), (1,))


def halves(value):
    high = value.astype(jnp.bfloat16)
    return high, (value - high.astype(jnp.float32)).astype(jnp.bfloat16)


def dot3(a, b, contract):
    return dot(a[0], b[0], contract) + (dot(a[0], b[1], contract) + dot(a[1], b[0], contract))


def eye(n):
    return jnp.where(
        lax.broadcasted_iota(jnp.int32, (n, n), 0) == lax.broadcasted_iota(jnp.int32, (n, n), 1), 1.0, 0.0
    ).astype(jnp.float32)


def inverse_factor(squares):
    n = squares.shape[0]
    wide = 2 * n
    step = ELIMINATE
    start = jnp.concatenate([squares, eye(n)], axis=1)
    rows = [start[i : i + step] for i in range(0, n, step)]
    below = lax.broadcasted_iota(jnp.int32, (step, wide), 0)
    for t in range(n // step):
        columns = [
            {i: jnp.broadcast_to(rows[i][:, t * step + j : t * step + j + 1], (step, wide)) for i in range(t, n // step)}
            for j in range(step)
        ]
        pivots = [rows[t][j : j + 1, :] for j in range(step)]
        update = {}
        for j in range(step):
            inverse = 1.0 / columns[j][t][j : j + 1, :]
            scaled = {i: columns[j][i] * inverse for i in range(t, n // step)}
            scaled[t] = jnp.where(below > j, scaled[t], 0.0)
            for i in range(t, n // step):
                term = scaled[i] * pivots[j]
                update[i] = update[i] + term if i in update else term
            for m in range(j + 1, step):
                pivots[m] = pivots[m] - scaled[t][m : m + 1, :] * pivots[j]
                across = columns[m][t][j : j + 1, :]
                for i in range(t, n // step):
                    columns[m][i] = columns[m][i] - scaled[i] * across
        for i in range(t, n // step):
            rows[i] = rows[i] - update[i]
    done = jnp.concatenate(rows, axis=0)
    left, right = done[:, :n], done[:, n:]
    diagonal = jnp.sum(left * eye(n), axis=1, keepdims=True)
    return right * lax.rsqrt(diagonal)


def extract_kernel(parts, which_ref, tensor_ref, out_ref, sems):
    rows = out_ref.shape[0] // parts
    copies = [
        pltpu.make_async_copy(
            tensor_ref.at[pl.ds(p * rows, rows), 0, which_ref[0], :], out_ref.at[pl.ds(p * rows, rows), :], sems.at[p]
        )
        for p in range(parts)
    ]
    for copy in copies:
        copy.start()
    for copy in copies:
        copy.wait()


def extract(which, tensor, parts=8):
    rows, width = tensor.shape[0], tensor.shape[3]
    return pl.pallas_call(
        functools.partial(extract_kernel, parts),
        out_shape=f32(rows, width),
        in_specs=[SMEM, ANY],
        out_specs=VMEM,
        scratch_shapes=[pltpu.SemaphoreType.DMA((parts,))],
        compiler_params=params(62),
        cost_estimate=pl.CostEstimate(flops=0, bytes_accessed=8 * rows * width, transcendentals=0),
        name="extract",
    )(which.reshape(1), tensor)


def arrive_kernel(before, last, *refs):
    piece_ref, basis_ref = refs[:2]
    old = refs[2 : 2 + 2 * before]
    state = refs[2 + 2 * before : 4 + 2 * before] if before else ()
    high_ref, low_ref, gram_ref, image_ref = refs[-4:]
    rows = piece_ref.shape[0]
    new = halves(piece_ref[...])
    high_ref[...], low_ref[...] = new
    every = tuple(
        jnp.concatenate([old[2 * k + s][...] for k in range(before)] + [new[s]], axis=0) for s in range(2)
    )
    block = dot3(new, every, NT)
    split = halves(block)
    basis = halves(basis_ref[:, : (before + 1) * rows])
    own = dot3(basis, split, NT)
    if not before:
        gram_ref[...] = block
        image_ref[...] = own
        return
    gram, image = state
    mine = tuple(b[:, before * rows :] for b in basis)
    earlier = dot3(mine, tuple(s[:, : before * rows] for s in split), NN)
    image_ref[...] = jnp.concatenate([image[...] + earlier, own], axis=1)
    if last:
        gram_ref[...] = block
    else:
        side = block[:, : before * rows]
        gram_ref[...] = jnp.concatenate(
            [jnp.concatenate([gram[...], side.T], axis=1), block], axis=0
        )


def arrive(before, last, piece, basis, old, state):
    rows, width = piece.shape
    ranks = basis.shape[0]
    size = (before + 1) * rows
    gram = f32(rows if last else size, size)
    return pl.pallas_call(
        functools.partial(arrive_kernel, before, last),
        out_shape=(bf16(rows, width), bf16(rows, width), gram, f32(ranks, size)),
        in_specs=[VMEM] * (2 + len(old) + len(state)),
        out_specs=(VMEM,) * 4,
        compiler_params=params(24),
        cost_estimate=pl.CostEstimate(
            flops=6 * rows * width * size, bytes_accessed=4 * width * size, transcendentals=0
        ),
        name="arrive",
    )(piece, basis, *old, *state)


def second_kernel(image_ref, gram_ref, block_ref, out_ref):
    head = gram_ref.shape[0]
    image = halves(image_ref[...])
    gram = halves(gram_ref[...])
    block = halves(block_ref[...])
    early = dot3(tuple(v[:, :head] for v in image), gram, NN)
    early = early + dot3(tuple(v[:, head:] for v in image), tuple(v[:, :head] for v in block), NN)
    late = dot3(image, block, NT)
    out_ref[...] = jnp.concatenate([early, late], axis=1)


def second(image, gram, block):
    return pl.pallas_call(
        second_kernel,
        out_shape=f32(*image.shape),
        in_specs=[VMEM] * 3,
        out_specs=VMEM,
        compiler_params=params(16),
        name="second",
    )(image, gram, block)


def factor_kernel(image_ref, out_ref):
    image = image_ref[...]
    out_ref[...] = inverse_factor(dot(image, image, NT, HIGHEST))


def factor(image):
    ranks = image.shape[0]
    return pl.pallas_call(
        factor_kernel,
        out_shape=f32(ranks, ranks),
        in_specs=[VMEM],
        out_specs=VMEM,
        compiler_params=params(8),
        cost_estimate=pl.CostEstimate(flops=40 * ranks**3, bytes_accessed=4 * image.size, transcendentals=0),
        name="factor",
    )(image)


def close_kernel(pieces, image_ref, inverse_ref, *refs):
    old, (core_ref, basis_ref, slab, sems) = refs[: 2 * pieces], refs[2 * pieces :]
    image = dot(inverse_ref[...], image_ref[...], NN, HIGHEST)
    parts = halves(image)
    inverse = inverse_factor(dot(image, image, NT, HIGHEST))
    width = old[0].shape[1]
    chunk = min(PROJECT, width)
    raw = []
    for c in range(0, width, chunk):
        columns = tuple(
            jnp.concatenate([old[2 * k + s][:, c : c + chunk] for k in range(pieces)], axis=0) for s in range(2)
        )
        raw.append(dot3(parts, columns, NN))
    basis_ref[...] = dot(inverse, image, NN, HIGHEST)
    split = halves(inverse)
    copies = []
    for n, c in enumerate(range(0, width, chunk)):
        slab[:, c : c + chunk] = dot3(split, halves(raw[n]), NN)
        copies.append(
            pltpu.make_async_copy(slab.at[:, pl.ds(c, chunk)], core_ref.at[:, 0, 0, pl.ds(c, chunk)], sems.at[n])
        )
        copies[-1].start()
    for copy in copies:
        copy.wait()


def close(image, inverse, old):
    ranks, modes = image.shape
    width = old[0].shape[1]
    return pl.pallas_call(
        functools.partial(close_kernel, len(old) // 2),
        out_shape=(f32(ranks, 1, 1, width), f32(ranks, modes)),
        in_specs=[VMEM] * (2 + len(old)),
        out_specs=(ANY, VMEM),
        scratch_shapes=[
            pltpu.VMEM((ranks, width), jnp.float32),
            pltpu.SemaphoreType.DMA((width // min(PROJECT, width),)),
        ],
        compiler_params=params(24),
        name="close",
    )(image, inverse, *old)


def swap(value, axis, size, bit):
    return lax.ppermute(value, axis, [(i, i ^ bit) for i in range(size)])


def bits(size):
    return [1 << b for b in range(size.bit_length() - 1)]


def block_order(value, blocks, bit):
    width = value.shape[1] // blocks
    parts = [value[:, k * width : (k + 1) * width] for k in range(blocks)]
    return jnp.concatenate([parts[k ^ bit] for k in range(blocks)], axis=1)


def total(value, n_fibre, n_cols):
    half = value.shape[0] // 2
    core = lax.axis_index("cols") % 2
    mine = lax.dynamic_slice_in_dim(value, core * half, half, 0)
    other = lax.dynamic_slice_in_dim(value, (1 - core) * half, half, 0)
    mine = mine + swap(other, "cols", n_cols, 1)
    for bit in bits(n_cols)[1:]:
        mine = mine + swap(mine, "cols", n_cols, bit)
    for bit in bits(n_fibre):
        mine = mine + block_order(swap(mine, "fibre", n_fibre, bit), n_fibre, bit)
    other = swap(mine, "cols", n_cols, 1)
    low = jnp.where(core == 0, mine, other)
    high = jnp.where(core == 0, other, mine)
    return jnp.concatenate([low, high], axis=0)


def shards(n_fibre, n_cols, tensor, initial):
    rows = tensor.shape[0]
    me = lax.axis_index("fibre")
    initial_t = initial.T
    start = jnp.concatenate(
        [lax.dynamic_slice_in_dim(initial_t, (me ^ k) * rows, rows, 1) for k in range(n_fibre)], axis=1
    )

    sent, token = {}, me
    for k in range(1, n_fibre):
        piece = extract(token ^ k, tensor)
        sent[k] = swap(piece, "fibre", n_fibre, k)
        token, _ = lax.optimization_barrier((me, piece))
    sent[0] = extract(token, tensor)

    old, state, gram, image = (), (), None, None
    for k in range(n_fibre):
        last = k == n_fibre - 1
        high, low, block, image = arrive(k, last, sent[k], start, old, state)
        old += (high, low)
        gram, state = (gram, state) if last else (block, (block, image))

    image = total(image, n_fibre, n_cols)
    inverse = factor(image)
    image = total(second(image, gram, block), n_fibre, n_cols)
    core_slab, basis_t = close(image, inverse, old)
    basis_t = jnp.concatenate(
        [lax.dynamic_slice_in_dim(basis_t, (me ^ k) * rows, rows, 1) for k in range(n_fibre)], axis=1
    )
    return (core_slab, basis_t.T)


def solution(mesh):
    n_fibre, n_cols = mesh.shape["fibre"], mesh.shape["cols"]
    placed = (P("fibre", "cols", None, None), P())
    return jax.shard_map(
        lambda tensor, initial: shards(n_fibre, n_cols, tensor, initial),
        mesh=mesh,
        in_specs=placed,
        out_specs=(P(None, "cols", "fibre", None), P()),
        check_vma=False,
    )
```

```python
import functools
import itertools

import jax
import jax.numpy as jnp
from jax import lax
from jax.experimental import pallas as pl
from jax.experimental.pallas import tpu as pltpu
from jax.sharding import PartitionSpec as P


HIGHEST = lax.Precision.HIGHEST
VMEM = pl.BlockSpec(memory_space=pltpu.VMEM)
ANY = pl.BlockSpec(memory_space=pl.ANY)
ELIMINATE = 8
PROJECT = 512


def params(mib):
    return pltpu.CompilerParams(vmem_limit_bytes=mib << 20)


def f32(*shape):
    return jax.ShapeDtypeStruct(shape, jnp.float32)


def bf16(*shape):
    return jax.ShapeDtypeStruct(shape, jnp.bfloat16)


def dot(a, b, contract, precision=None):
    return lax.dot_general(
        a, b, (contract, ((), ())), precision=precision, preferred_element_type=jnp.float32
    )


NN = ((1,), (0,))
NT = ((1,), (1,))


def halves(value):
    high = value.astype(jnp.bfloat16)
    return high, (value - high.astype(jnp.float32)).astype(jnp.bfloat16)


def dot3(a, b, contract):
    return dot(a[0], b[0], contract) + (dot(a[0], b[1], contract) + dot(a[1], b[0], contract))


def eye(n):
    return jnp.where(
        lax.broadcasted_iota(jnp.int32, (n, n), 0) == lax.broadcasted_iota(jnp.int32, (n, n), 1), 1.0, 0.0
    ).astype(jnp.float32)


def inverse_factor(squares):
    n = squares.shape[0]
    wide = 2 * n
    step = ELIMINATE
    start = jnp.concatenate([squares, eye(n)], axis=1)
    rows = [start[i : i + step] for i in range(0, n, step)]
    below = lax.broadcasted_iota(jnp.int32, (step, wide), 0)
    for t in range(n // step):
        columns = [
            {i: jnp.broadcast_to(rows[i][:, t * step + j : t * step + j + 1], (step, wide)) for i in range(t, n // step)}
            for j in range(step)
        ]
        pivots = [rows[t][j : j + 1, :] for j in range(step)]
        update = {}
        for j in range(step):
            inverse = 1.0 / columns[j][t][j : j + 1, :]
            scaled = {i: columns[j][i] * inverse for i in range(t, n // step)}
            scaled[t] = jnp.where(below > j, scaled[t], 0.0)
            for i in range(t, n // step):
                term = scaled[i] * pivots[j]
                update[i] = update[i] + term if i in update else term
            for m in range(j + 1, step):
                pivots[m] = pivots[m] - scaled[t][m : m + 1, :] * pivots[j]
                across = columns[m][t][j : j + 1, :]
                for i in range(t, n // step):
                    columns[m][i] = columns[m][i] - scaled[i] * across
        for i in range(t, n // step):
            rows[i] = rows[i] - update[i]
    done = jnp.concatenate(rows, axis=0)
    left, right = done[:, :n], done[:, n:]
    diagonal = jnp.sum(left * eye(n), axis=1, keepdims=True)
    return right * lax.rsqrt(diagonal)


def extract_kernel(shift, column, tensor_ref, out_ref, sem):
    width = out_ref.shape[1]
    which = lax.axis_index("fibre") ^ shift
    copy = pltpu.make_async_copy(tensor_ref.at[:, 0, which, pl.ds(column, width)], out_ref, sem)
    copy.start()
    copy.wait()


def extract(shift, tensor, column, width):
    rows = tensor.shape[0]
    return pl.pallas_call(
        functools.partial(extract_kernel, shift, column),
        out_shape=f32(rows, width),
        in_specs=[ANY],
        out_specs=VMEM,
        scratch_shapes=[pltpu.SemaphoreType.DMA(())],
        compiler_params=params(62),
        cost_estimate=pl.CostEstimate(flops=0, bytes_accessed=8 * rows * width, transcendentals=0),
        name="extract",
    )(tensor)


def cross(every, new):
    size, rows = every[0].shape[0], new[0].shape[0]
    full = dot(jnp.concatenate(every, axis=0), jnp.concatenate(new, axis=0), NT)
    return full[:size, :rows] + (full[:size, rows:] + full[size:, :rows] + full[size:, rows:])


def joined(refs, columns=slice(None)):
    return tuple(jnp.concatenate([refs[k + s][:, columns] for k in range(0, len(refs), 2)], axis=0) for s in range(2))


def in_turn(ref, shifts):
    me = lax.axis_index("fibre")
    return jnp.concatenate([ref[me ^ shift] for shift in shifts], axis=1)


def low_core():
    return lax.axis_index("cols") % 2 == 0


def put(value, shifts, mine_ref, other_ref):
    me = lax.axis_index("fibre")
    half, rows = mine_ref.shape[1:]
    low, high = value[:half], value[half:]
    mine, other = jnp.where(low_core(), low, high), jnp.where(low_core(), high, low)
    for p, shift in enumerate(shifts):
        mine_ref[me ^ shift] = mine[:, p * rows : (p + 1) * rows]
        other_ref[me ^ shift] = other[:, p * rows : (p + 1) * rows]


def merged(mine, other):
    return jnp.concatenate([jnp.where(low_core(), mine, other), jnp.where(low_core(), other, mine)], axis=0)


def by_fibre(ref):
    return jnp.concatenate([ref[f] for f in range(ref.shape[0])], axis=1)


def arrive_kernel(parts, shifts, *refs):
    before = len(shifts) - 1
    piece = jnp.concatenate([ref[...] for ref in refs[:parts]], axis=1)
    basis_ref = refs[parts]
    old = refs[parts + 1 : parts + 1 + 2 * before]
    high_ref, low_ref, gram_ref, image_ref = refs[-4:]
    rows = piece.shape[0]
    new = halves(piece)
    high_ref[...], low_ref[...] = new
    if not before:
        every = new
    else:
        every = tuple(jnp.concatenate(pair, axis=0) for pair in zip(joined(old), new))
    column = cross(every, new)
    split = halves(column)
    basis = halves(in_turn(basis_ref, shifts))
    own = dot3(basis, split, NN)
    if not before:
        gram_ref[...] = column
        image_ref[...] = own
        return
    gram, image = refs[parts + 1 + 2 * before :][:2]
    side = before * rows
    mine = tuple(b[:, side:] for b in basis)
    earlier = dot3(mine, tuple(s[:side] for s in split), NT)
    image_ref[...] = jnp.concatenate([image[...] + earlier, own], axis=1)
    gram_ref[...] = jnp.concatenate(
        [jnp.concatenate([gram[...], column[:side].T], axis=0), column], axis=1
    )


def arrive(parts, shifts, basis, old, state):
    rows, width = parts[0].shape[0], sum(part.shape[1] for part in parts)
    size = len(shifts) * rows
    return pl.pallas_call(
        functools.partial(arrive_kernel, len(parts), shifts),
        out_shape=(bf16(rows, width), bf16(rows, width), f32(size, size), f32(basis.shape[1], size)),
        in_specs=[VMEM] * (len(parts) + 1 + len(old) + len(state)),
        out_specs=(VMEM,) * 4,
        compiler_params=params(24),
        cost_estimate=pl.CostEstimate(
            flops=8 * rows * width * size, bytes_accessed=4 * width * size, transcendentals=0
        ),
        name="arrive",
    )(*parts, basis, *old, *state)


def partial_kernel(start, *refs):
    piece_ref, old, (high_ref, low_ref, out_ref) = refs[0], refs[1:-3], refs[-3:]
    new = halves(piece_ref[...])
    high_ref[...], low_ref[...] = new
    every = tuple(
        jnp.concatenate(pair, axis=0) for pair in zip(joined(old, slice(start, start + new[0].shape[1])), new)
    )
    out_ref[...] = cross(every, new)


def partial_column(part, start, old):
    rows, width = part.shape
    size = (len(old) // 2 + 1) * rows
    return pl.pallas_call(
        functools.partial(partial_kernel, start),
        out_shape=(bf16(rows, width), bf16(rows, width), f32(size, rows)),
        in_specs=[VMEM] * (1 + len(old)),
        out_specs=(VMEM,) * 3,
        compiler_params=params(24),
        cost_estimate=pl.CostEstimate(
            flops=8 * rows * width * size, bytes_accessed=4 * width * size, transcendentals=0
        ),
        name="partial",
    )(part, *old)


def finish_kernel(start, shifts, piece_ref, basis_ref, image_ref, sofar_ref, *refs):
    old, (high_ref, low_ref, column_ref, mine_ref, other_ref) = refs[:-5], refs[-5:]
    rows = piece_ref.shape[0]
    new = halves(piece_ref[...])
    high_ref[...], low_ref[...] = new
    every = tuple(
        jnp.concatenate(pair, axis=0) for pair in zip(joined(old, slice(start, start + new[0].shape[1])), new)
    )
    column = sofar_ref[...] + cross(every, new)
    column_ref[...] = column
    side = column.shape[0] - rows
    split = halves(column)
    basis = halves(in_turn(basis_ref, shifts))
    own = dot3(basis, split, NN)
    earlier = image_ref[...] + dot3(tuple(b[:, side:] for b in basis), tuple(s[:side] for s in split), NT)
    put(jnp.concatenate([earlier, own], axis=1), shifts, mine_ref, other_ref)


def finish(part, start, shifts, basis, image, sofar, old):
    rows, width = part.shape
    size = sofar.shape[0]
    share = f32(len(shifts), basis.shape[1] // 2, rows)
    return pl.pallas_call(
        functools.partial(finish_kernel, start, shifts),
        out_shape=(bf16(rows, width), bf16(rows, width), f32(size, rows), share, share),
        in_specs=[VMEM] * (4 + len(old)),
        out_specs=(VMEM,) * 5,
        compiler_params=params(24),
        cost_estimate=pl.CostEstimate(
            flops=8 * rows * width * size, bytes_accessed=4 * width * size, transcendentals=0
        ),
        name="finish",
    )(part, basis, image, sofar, *old)


def second_kernel(shifts, mine_ref, other_ref, gram_ref, column_ref, to_mine_ref, to_other_ref):
    side = gram_ref.shape[0]
    image = halves(merged(in_turn(mine_ref, shifts), in_turn(other_ref, shifts)))
    gram = halves(gram_ref[...])
    column = halves(column_ref[...])
    late = dot3(image, column, NN)
    early = dot3(tuple(v[:, :side] for v in image), gram, NN)
    early = early + dot3(tuple(v[:, side:] for v in image), tuple(v[:side] for v in column), NT)
    put(jnp.concatenate([early, late], axis=1), shifts, to_mine_ref, to_other_ref)


def second(shifts, mine, other, gram, column):
    return pl.pallas_call(
        functools.partial(second_kernel, shifts),
        out_shape=(f32(*mine.shape), f32(*mine.shape)),
        in_specs=[VMEM] * 4,
        out_specs=(VMEM,) * 2,
        compiler_params=params(16),
        name="second",
    )(mine, other, gram, column)


def factor_kernel(mine_ref, other_ref, out_ref):
    image = merged(by_fibre(mine_ref), by_fibre(other_ref))
    out_ref[...] = inverse_factor(dot(image, image, NT, HIGHEST))


def factor(mine, other):
    ranks = 2 * mine.shape[1]
    return pl.pallas_call(
        factor_kernel,
        out_shape=f32(ranks, ranks),
        in_specs=[VMEM] * 2,
        out_specs=VMEM,
        compiler_params=params(8),
        cost_estimate=pl.CostEstimate(flops=40 * ranks**3, bytes_accessed=8 * mine.size, transcendentals=0),
        name="factor",
    )(mine, other)


def close_kernel(places, shifts, mine_ref, other_ref, inverse_ref, *refs):
    pieces, (core_ref, basis_ref, slab, sems) = refs[: 2 * len(places)], refs[2 * len(places) :]
    first = inverse_ref[...]
    image = dot(first, merged(by_fibre(mine_ref), by_fibre(other_ref)), NN, HIGHEST)
    turned = dot(first, merged(in_turn(mine_ref, shifts), in_turn(other_ref, shifts)), NN, HIGHEST)
    parts = halves(turned)
    inverse = inverse_factor(dot(image, image, NT, HIGHEST))
    width = core_ref.shape[3]
    chunk = min(PROJECT, width)
    raw = []
    for c in range(0, width, chunk):
        cut = [
            i for p in range(len(shifts)) for i, (q, at) in enumerate(places)
            if q == p and at <= c < at + pieces[2 * i].shape[1]
        ]
        columns = tuple(
            jnp.concatenate([pieces[2 * i + s][:, c - places[i][1] : c - places[i][1] + chunk] for i in cut], axis=0)
            for s in range(2)
        )
        raw.append(dot3(parts, columns, NN))
    basis_ref[...] = dot(inverse, image, NN, HIGHEST)
    split = halves(inverse)
    stores = []
    for n, c in enumerate(range(0, width, chunk)):
        slab[:, c : c + chunk] = dot3(split, halves(raw[n]), NN)
        stores.append(
            pltpu.make_async_copy(slab.at[:, pl.ds(c, chunk)], core_ref.at[:, 0, 0, pl.ds(c, chunk)], sems.at[n])
        )
        stores[-1].start()
    for store in stores:
        store.wait()


def close(shifts, mine, other, inverse, pieces, places, width):
    fibres, half, rows = mine.shape
    return pl.pallas_call(
        functools.partial(close_kernel, places, shifts),
        out_shape=(f32(2 * half, 1, 1, width), f32(2 * half, fibres * rows)),
        in_specs=[VMEM] * (3 + len(pieces)),
        out_specs=(ANY, VMEM),
        scratch_shapes=[
            pltpu.VMEM((2 * half, width), jnp.float32),
            pltpu.SemaphoreType.DMA((width // min(PROJECT, width),)),
        ],
        compiler_params=params(24),
        name="close",
    )(mine, other, inverse, *pieces)


def swap(value, axis, size, bit):
    return lax.ppermute(value, axis, [(i, i ^ bit) for i in range(size)])


def bits(size):
    return [1 << b for b in range(size.bit_length() - 1)]


def chips(n_fibre, n_cols):
    moves = [(0, bit) for bit in bits(n_cols)[1:]], [(bit, 0) for bit in bits(n_fibre)]
    return [axis[i : i + 2] for axis in moves for i in range(0, len(axis), 2)]


def across(value, n_fibre, n_cols, flip):
    perm = [
        (f * n_cols + c, (f ^ flip[0]) * n_cols + (c ^ flip[1])) for f in range(n_fibre) for c in range(n_cols)
    ]
    return lax.ppermute(value, ("fibre", "cols"), perm)


def total(mine, other, n_fibre, n_cols):
    mine = mine + swap(other, "cols", n_cols, 1)
    for flips in chips(n_fibre, n_cols):
        if len(flips) == 1:
            mine = mine + across(mine, n_fibre, n_cols, flips[0])
            continue
        both = (flips[0][0] ^ flips[1][0], flips[0][1] ^ flips[1][1])
        one, two, three = (across(mine, n_fibre, n_cols, flip) for flip in (*flips, both))
        mine = (mine + one) + (two + three)
    return mine, swap(mine, "cols", n_cols, 1)


def turns(n_fibre):
    images = [n_fibre - 1] + bits(n_fibre)[:-1]
    out = []
    for p in range(n_fibre):
        shift = 0
        for b, image in enumerate(images):
            shift ^= image if p >> b & 1 else 0
        out.append(shift)
    return out


def shards(n_fibre, n_cols, tensor, initial):
    rows, width = tensor.shape[0], tensor.shape[3]
    shifts = turns(n_fibre)
    start = initial.reshape(n_fibre, rows, initial.shape[1]).transpose(0, 2, 1)

    tail = width - width // 4
    last = n_fibre - 1
    cuts = {1: (0, width // 2, width), last: (0, tail, width)}
    parts, sends = {}, 0
    for p in [*range(1, last), 0, last]:
        parts[p] = []
        for c, end in itertools.pairwise(cuts.get(p, (0, width))):
            part = extract(shifts[p], tensor, c, end - c)
            if p:
                part = swap(part, "fibre", n_fibre, shifts[p])
                sends += 1
            parts[p].append(part)

    old, state, places = (), (), []
    for p in range(last):
        high, low, gram, image = arrive(parts[p], shifts[: p + 1], start, old, state)
        old += (high, low)
        state = (gram, image)
        places.append((p, 0))
    high, low, column = partial_column(parts[last][0], 0, old)
    *ends, column, mine, other = finish(parts[last][1], tail, shifts, start, image, column, old)
    pieces = (*old, high, low, *ends)
    places += [(last, 0), (last, tail)]

    mine, other = total(mine, other, n_fibre, n_cols)
    inverse = factor(mine, other)
    mine, other = total(*second(shifts, mine, other, gram, column), n_fibre, n_cols)
    core_slab, basis_t = close(shifts, mine, other, inverse, pieces, places, width)
    return (core_slab, basis_t.T)


def solution(mesh):
    n_fibre, n_cols = mesh.shape["fibre"], mesh.shape["cols"]
    placed = (P("fibre", "cols", None, None), P())

    def body(tensor, initial):
        return shards(n_fibre, n_cols, tensor, initial)

    return jax.shard_map(
        body,
        mesh=mesh,
        in_specs=placed,
        out_specs=(P(None, "cols", "fibre", None), P()),
        check_vma=False,
    )
```

```python
import functools
import itertools

import jax
import jax.numpy as jnp
from jax import lax
from jax.experimental import pallas as pl
from jax.experimental.pallas import tpu as pltpu
from jax.sharding import PartitionSpec as P


HIGHEST = lax.Precision.HIGHEST
VMEM = pl.BlockSpec(memory_space=pltpu.VMEM)
ANY = pl.BlockSpec(memory_space=pl.ANY)
ELIMINATE = 8
PROJECT = 512


def params(mib):
    return pltpu.CompilerParams(vmem_limit_bytes=mib << 20)


def f32(*shape):
    return jax.ShapeDtypeStruct(shape, jnp.float32)


def bf16(*shape):
    return jax.ShapeDtypeStruct(shape, jnp.bfloat16)


def dot(a, b, contract, precision=None):
    return lax.dot_general(
        a, b, (contract, ((), ())), precision=precision, preferred_element_type=jnp.float32
    )


NN = ((1,), (0,))
NT = ((1,), (1,))


def halves(value):
    high = value.astype(jnp.bfloat16)
    return high, (value - high.astype(jnp.float32)).astype(jnp.bfloat16)


def dot3(a, b, contract):
    return dot(a[0], b[0], contract) + (dot(a[0], b[1], contract) + dot(a[1], b[0], contract))


def eye(n):
    return jnp.where(
        lax.broadcasted_iota(jnp.int32, (n, n), 0) == lax.broadcasted_iota(jnp.int32, (n, n), 1), 1.0, 0.0
    ).astype(jnp.float32)


def inverse_factor(squares):
    n = squares.shape[0]
    wide = 2 * n
    step = ELIMINATE
    start = jnp.concatenate([squares, eye(n)], axis=1)
    rows = [start[i : i + step] for i in range(0, n, step)]
    below = lax.broadcasted_iota(jnp.int32, (step, wide), 0)
    for t in range(n // step):
        columns = [
            {i: jnp.broadcast_to(rows[i][:, t * step + j : t * step + j + 1], (step, wide)) for i in range(t, n // step)}
            for j in range(step)
        ]
        pivots = [rows[t][j : j + 1, :] for j in range(step)]
        update = {}
        for j in range(step):
            inverse = 1.0 / columns[j][t][j : j + 1, :]
            scaled = {i: columns[j][i] * inverse for i in range(t, n // step)}
            scaled[t] = jnp.where(below > j, scaled[t], 0.0)
            for i in range(t, n // step):
                term = scaled[i] * pivots[j]
                update[i] = update[i] + term if i in update else term
            for m in range(j + 1, step):
                pivots[m] = pivots[m] - scaled[t][m : m + 1, :] * pivots[j]
                across = columns[m][t][j : j + 1, :]
                for i in range(t, n // step):
                    columns[m][i] = columns[m][i] - scaled[i] * across
        for i in range(t, n // step):
            rows[i] = rows[i] - update[i]
    done = jnp.concatenate(rows, axis=0)
    left, right = done[:, :n], done[:, n:]
    diagonal = jnp.sum(left * eye(n), axis=1, keepdims=True)
    return right * lax.rsqrt(diagonal)


def extract_kernel(shift, row, tensor_ref, out_ref, sem):
    rows = out_ref.shape[0]
    which = lax.axis_index("fibre") ^ shift
    copy = pltpu.make_async_copy(tensor_ref.at[pl.ds(row, rows), 0, which, :], out_ref, sem)
    copy.start()
    copy.wait()


def extract(shift, tensor, row, rows):
    width = tensor.shape[3]
    return pl.pallas_call(
        functools.partial(extract_kernel, shift, row),
        out_shape=f32(rows, width),
        in_specs=[ANY],
        out_specs=VMEM,
        scratch_shapes=[pltpu.SemaphoreType.DMA(())],
        compiler_params=params(62),
        cost_estimate=pl.CostEstimate(flops=0, bytes_accessed=8 * rows * width, transcendentals=0),
        name="extract",
    )(tensor)


def cross(every, new):
    size, rows = every[0].shape[0], new[0].shape[0]
    full = dot(jnp.concatenate(every, axis=0), jnp.concatenate(new, axis=0), NT)
    return full[:size, :rows] + (full[:size, rows:] + full[size:, :rows] + full[size:, rows:])


def joined(refs):
    return [jnp.concatenate([ref[...] for ref in refs[s::2]], axis=0) for s in range(2)]


def low_core():
    return lax.axis_index("cols") % 2 == 0


def shares(value):
    half = value.shape[0] // 2
    low, high = value[:half], value[half:]
    return jnp.where(low_core(), low, high), jnp.where(low_core(), high, low)


def merged(mine, other):
    return jnp.concatenate([jnp.where(low_core(), mine, other), jnp.where(low_core(), other, mine)], axis=0)


def in_turn(ref, shifts):
    me = lax.axis_index("fibre")
    return jnp.concatenate([ref[me ^ shift] for shift in shifts], axis=1)


def by_fibre(ref):
    return jnp.concatenate([ref[f] for f in range(ref.shape[0])], axis=1)


def put(value, shifts, ref):
    me, rows = lax.axis_index("fibre"), ref.shape[2]
    for p, shift in enumerate(shifts):
        ref[me ^ shift] = value[:, p * rows : (p + 1) * rows]


def arrive_kernel(parts, before, share, *refs):
    piece = jnp.concatenate([ref[...] for ref in refs[:parts]], axis=0)
    old = refs[parts : parts + 2 * before]
    state = refs[parts + 2 * before : parts + 2 * before + bool(before)]
    high_ref, low_ref, *gram_refs = refs[parts + 2 * before + bool(before) :]
    new = halves(piece)
    high_ref[...], low_ref[...] = new
    if before:
        column = cross([jnp.concatenate(pair, axis=0) for pair in zip(joined(old), new)], new)
        side = state[0].shape[0]
        gram = jnp.concatenate([jnp.concatenate([state[0][...], column[:side].T], axis=0), column], axis=1)
    else:
        gram = cross(new, new)
    for ref, value in zip(gram_refs, shares(gram) if share else [gram]):
        ref[...] = value


def arrive(parts, old, state, share):
    rows, width = sum(part.shape[0] for part in parts), parts[0].shape[1]
    size = sum(piece.shape[0] for piece in old[::2]) + rows
    out = (bf16(rows, width),) * 2 + ((f32(size // 2, size),) * 2 if share else (f32(size, size),))
    return pl.pallas_call(
        functools.partial(arrive_kernel, len(parts), len(old) // 2, share),
        out_shape=out,
        in_specs=[VMEM] * (len(parts) + len(old) + len(state)),
        out_specs=(VMEM,) * len(out),
        compiler_params=params(24),
        cost_estimate=pl.CostEstimate(
            flops=8 * rows * width * size, bytes_accessed=4 * width * size, transcendentals=0
        ),
        name="arrive",
    )(*parts, *old, *state)


def stripe_kernel(piece_ref, *refs):
    old, (high_ref, low_ref, mine_ref, other_ref) = refs[:-4], refs[-4:]
    new = halves(piece_ref[...])
    high_ref[...], low_ref[...] = new
    column = cross([jnp.concatenate(pair, axis=0) for pair in zip(joined(old), new)], new)
    mine_ref[...], other_ref[...] = shares(column.T)


def stripe(part, old):
    rows, width = part.shape
    size = sum(piece.shape[0] for piece in old[::2]) + rows
    return pl.pallas_call(
        stripe_kernel,
        out_shape=(bf16(rows, width),) * 2 + (f32(rows // 2, size),) * 2,
        in_specs=[VMEM] * (1 + len(old)),
        out_specs=(VMEM,) * 4,
        compiler_params=params(24),
        cost_estimate=pl.CostEstimate(
            flops=8 * rows * width * size, bytes_accessed=4 * width * size, transcendentals=0
        ),
        name="stripe",
    )(part, *old)


def ranks_here(basis):
    half = basis.shape[0] // 2
    return jnp.where(low_core(), basis[:half], basis[half:])


def assemble_kernel(shifts, basis_ref, gram_mine, gram_other, mine_ref, other_ref, high_ref, low_ref, image_ref):
    block = merged(gram_mine[...], gram_other[...])
    lower = merged(mine_ref[...], other_ref[...])
    side = block.shape[0]
    gram = jnp.concatenate(
        [jnp.concatenate([block, lower[:, :side]], axis=0), lower.T], axis=1
    )
    split = halves(gram)
    high_ref[...], low_ref[...] = split
    basis = halves(ranks_here(in_turn(basis_ref, shifts))[:, : gram.shape[0]])
    image_ref[...] = dot3(basis, split, NN)


def assemble(shifts, basis, block, lower):
    size = lower[0].shape[1]
    return pl.pallas_call(
        functools.partial(assemble_kernel, shifts),
        out_shape=(bf16(size, size), bf16(size, size), f32(basis.shape[1] // 2, size)),
        in_specs=[VMEM] * 5,
        out_specs=(VMEM,) * 3,
        compiler_params=params(16),
        name="assemble",
    )(basis, *block, *lower)


def with_stripe(early, image, stripe):
    side = stripe[0].shape[1] - stripe[0].shape[0]
    late = dot3(image, stripe, NT)
    early = early + dot3([v[:, side:] for v in image], [v[:, :side] for v in stripe], NN)
    return jnp.concatenate([early, late], axis=1)


def first_kernel(shifts, basis_ref, image_ref, mine_ref, other_ref, out_ref):
    basis = halves(ranks_here(in_turn(basis_ref, shifts)))
    put(with_stripe(image_ref[...], basis, halves(merged(mine_ref[...], other_ref[...]))), shifts, out_ref)


def first(shifts, basis, image, stripe):
    fibres, ranks, rows = basis.shape
    return pl.pallas_call(
        functools.partial(first_kernel, shifts),
        out_shape=f32(fibres, ranks // 2, rows),
        in_specs=[VMEM] * 4,
        out_specs=VMEM,
        compiler_params=params(16),
        name="first",
    )(basis, image, *stripe)


def second_kernel(shifts, image_ref, high_ref, low_ref, mine_ref, other_ref, out_ref):
    image = halves(in_turn(image_ref, shifts))
    side = high_ref.shape[0]
    early = dot3([v[:, :side] for v in image], (high_ref[...], low_ref[...]), NN)
    put(with_stripe(early, image, halves(merged(mine_ref[...], other_ref[...]))), shifts, out_ref)


def second(shifts, image, gram, stripe):
    return pl.pallas_call(
        functools.partial(second_kernel, shifts),
        out_shape=f32(*image.shape),
        in_specs=[VMEM] * 5,
        out_specs=VMEM,
        compiler_params=params(16),
        name="second",
    )(image, *gram, *stripe)


def factor_kernel(mine_ref, other_ref, out_ref):
    image = merged(by_fibre(mine_ref), by_fibre(other_ref))
    out_ref[...] = inverse_factor(dot(image, image, NT, HIGHEST))


def factor(mine, other):
    ranks = 2 * mine.shape[1]
    return pl.pallas_call(
        factor_kernel,
        out_shape=f32(ranks, ranks),
        in_specs=[VMEM] * 2,
        out_specs=VMEM,
        compiler_params=params(8),
        cost_estimate=pl.CostEstimate(flops=40 * ranks**3, bytes_accessed=8 * mine.size, transcendentals=0),
        name="factor",
    )(mine, other)


def close_kernel(shifts, mine_ref, other_ref, inverse_ref, *refs):
    pieces, (core_ref, basis_ref, slab, sems) = refs[:-4], refs[-4:]
    first = inverse_ref[...]
    image = dot(first, merged(by_fibre(mine_ref), by_fibre(other_ref)), NN, HIGHEST)
    turned = dot(first, merged(in_turn(mine_ref, shifts), in_turn(other_ref, shifts)), NN, HIGHEST)
    parts = halves(turned)
    inverse = inverse_factor(dot(image, image, NT, HIGHEST))
    width = core_ref.shape[3]
    chunk = min(PROJECT, width)
    raw = []
    for c in range(0, width, chunk):
        columns = [jnp.concatenate([ref[:, c : c + chunk] for ref in pieces[k::2]], axis=0) for k in range(2)]
        raw.append(dot3(parts, columns, NN))
    basis_ref[...] = dot(inverse, image, NN, HIGHEST)
    split = halves(inverse)
    stores = []
    for n, c in enumerate(range(0, width, chunk)):
        slab[:, c : c + chunk] = dot3(split, halves(raw[n]), NN)
        stores.append(
            pltpu.make_async_copy(slab.at[:, pl.ds(c, chunk)], core_ref.at[:, 0, 0, pl.ds(c, chunk)], sems.at[n])
        )
        stores[-1].start()
    for store in stores:
        store.wait()


def close(shifts, mine, other, inverse, pieces):
    fibres, half, rows = mine.shape
    width = pieces[0].shape[1]
    return pl.pallas_call(
        functools.partial(close_kernel, shifts),
        out_shape=(f32(2 * half, 1, 1, width), f32(2 * half, fibres * rows)),
        in_specs=[VMEM] * (3 + len(pieces)),
        out_specs=(ANY, VMEM),
        scratch_shapes=[
            pltpu.VMEM((2 * half, width), jnp.float32),
            pltpu.SemaphoreType.DMA((width // min(PROJECT, width),)),
        ],
        compiler_params=params(24),
        name="close",
    )(mine, other, inverse, *pieces)


def swap(value, axis, size, bit):
    return lax.ppermute(value, axis, [(i, i ^ bit) for i in range(size)])


def bits(size):
    return [1 << b for b in range(size.bit_length() - 1)]


def crossings(flips):
    return [flips[i : i + 2] for i in range(0, len(flips), 2)]


def over_chips(value, axis, size):
    for flips in crossings(bits(size)[axis == "cols" :]):
        if len(flips) == 1:
            value = value + swap(value, axis, size, flips[0])
            continue
        one, two, three = (swap(value, axis, size, flip) for flip in (*flips, flips[0] ^ flips[1]))
        value = (value + one) + (two + three)
    return value


def over_cols(mine, other, n_cols):
    mine = over_chips(mine + swap(other, "cols", n_cols, 1), "cols", n_cols)
    return mine, swap(mine, "cols", n_cols, 1)


def turns(n_fibre):
    images = [n_fibre - 1] + bits(n_fibre)[:-1]
    out = []
    for p in range(n_fibre):
        shift = 0
        for b, image in enumerate(images):
            shift ^= image if p >> b & 1 else 0
        out.append(shift)
    return out


def shards(n_fibre, n_cols, tensor, initial):
    rows = tensor.shape[0]
    shifts = turns(n_fibre)
    start = initial.reshape(n_fibre, rows, initial.shape[1]).transpose(0, 2, 1)

    last = n_fibre - 1
    cuts = {1: (0, rows // 2, rows), last: (0, rows // 2, rows)}
    parts, sends = {}, 0
    for p in [*range(1, last), 0, last]:
        parts[p] = []
        for row, end in itertools.pairwise(cuts.get(p, (0, rows))):
            part = extract(shifts[p], tensor, row, end - row)
            if p:
                part = swap(part, "fibre", n_fibre, shifts[p])
                sends += 1
            parts[p].append(part)

    pieces, state = (), ()
    for p in range(last):
        high, low, *state = arrive(parts[p], pieces, state, p == last - 1)
        pieces += (high, low)
    block = over_cols(*state, n_cols)
    high, low, *lower = stripe(parts[last][0], pieces)
    pieces += (high, low)
    lower = over_cols(*lower, n_cols)
    *gram, image = assemble(shifts, start, block, lower)
    high, low, *lower = stripe(parts[last][1], pieces)
    pieces += (high, low)
    lower = over_cols(*lower, n_cols)

    mine = over_chips(first(shifts, start, image, lower), "fibre", n_fibre)
    other = swap(mine, "cols", n_cols, 1)
    inverse = factor(mine, other)
    mine = second(shifts, mine, gram, lower)
    mine = over_chips(mine, "fibre", n_fibre)
    core_slab, basis_t = close(shifts, mine, swap(mine, "cols", n_cols, 1), inverse, pieces)
    return (core_slab, basis_t.T)


def solution(mesh):
    n_fibre, n_cols = mesh.shape["fibre"], mesh.shape["cols"]
    placed = (P("fibre", "cols", None, None), P())

    def body(tensor, initial):
        return shards(n_fibre, n_cols, tensor, initial)

    return jax.shard_map(
        body,
        mesh=mesh,
        in_specs=placed,
        out_specs=(P(None, "cols", "fibre", None), P()),
        check_vma=False,
    )
```

```python
import functools
import itertools

import jax
import jax.numpy as jnp
from jax import lax
from jax.experimental import pallas as pl
from jax.experimental.pallas import tpu as pltpu
from jax.sharding import PartitionSpec as P


HIGHEST = lax.Precision.HIGHEST
VMEM = pl.BlockSpec(memory_space=pltpu.VMEM)
ANY = pl.BlockSpec(memory_space=pl.ANY)
ELIMINATE = 8
PROJECT = 256


def params(mib):
    return pltpu.CompilerParams(vmem_limit_bytes=mib << 20)


def f32(*shape):
    return jax.ShapeDtypeStruct(shape, jnp.float32)


def bf16(*shape):
    return jax.ShapeDtypeStruct(shape, jnp.bfloat16)


def dot(a, b, contract, precision=None):
    return lax.dot_general(
        a, b, (contract, ((), ())), precision=precision, preferred_element_type=jnp.float32
    )


NN = ((1,), (0,))
NT = ((1,), (1,))


def halves(value):
    high = value.astype(jnp.bfloat16)
    return high, (value - high.astype(jnp.float32)).astype(jnp.bfloat16)


def dot3(a, b, contract):
    return dot(a[0], b[0], contract) + (dot(a[0], b[1], contract) + dot(a[1], b[0], contract))


def eye(n):
    return jnp.where(
        lax.broadcasted_iota(jnp.int32, (n, n), 0) == lax.broadcasted_iota(jnp.int32, (n, n), 1), 1.0, 0.0
    ).astype(jnp.float32)


def inverse_factor(squares, beside=()):
    n = squares.shape[0]
    wide = 2 * n
    step = ELIMINATE
    start = jnp.concatenate([squares, eye(n)], axis=1)
    rows = [start[i : i + step] for i in range(0, n, step)]
    below = lax.broadcasted_iota(jnp.int32, (step, wide), 0)
    beside = list(beside)
    for t in range(n // step):
        if beside:
            beside.pop(0)()
        columns = [
            {i: jnp.broadcast_to(rows[i][:, t * step + j : t * step + j + 1], (step, wide)) for i in range(t, n // step)}
            for j in range(step)
        ]
        pivots = [rows[t][j : j + 1, :] for j in range(step)]
        update = {}
        for j in range(step):
            inverse = 1.0 / columns[j][t][j : j + 1, :]
            scaled = {i: columns[j][i] * inverse for i in range(t, n // step)}
            scaled[t] = jnp.where(below > j, scaled[t], 0.0)
            for i in range(t, n // step):
                term = scaled[i] * pivots[j]
                update[i] = update[i] + term if i in update else term
            for m in range(j + 1, step):
                pivots[m] = pivots[m] - scaled[t][m : m + 1, :] * pivots[j]
                across = columns[m][t][j : j + 1, :]
                for i in range(t, n // step):
                    columns[m][i] = columns[m][i] - scaled[i] * across
        for i in range(t, n // step):
            rows[i] = rows[i] - update[i]
    for call in beside:
        call()
    done = jnp.concatenate(rows, axis=0)
    left, right = done[:, :n], done[:, n:]
    diagonal = jnp.sum(left * eye(n), axis=1, keepdims=True)
    return right * lax.rsqrt(diagonal)


def extract_kernel(shift, row, tensor_ref, out_ref, sem):
    rows = out_ref.shape[0]
    which = lax.axis_index("fibre") ^ shift
    copy = pltpu.make_async_copy(tensor_ref.at[pl.ds(row, rows), 0, which, :], out_ref, sem)
    copy.start()
    copy.wait()


def extract(shift, tensor, row, rows):
    width = tensor.shape[3]
    return pl.pallas_call(
        functools.partial(extract_kernel, shift, row),
        out_shape=f32(rows, width),
        in_specs=[ANY],
        out_specs=VMEM,
        scratch_shapes=[pltpu.SemaphoreType.DMA(())],
        compiler_params=params(62),
        cost_estimate=pl.CostEstimate(flops=0, bytes_accessed=8 * rows * width, transcendentals=0),
        name="extract",
    )(tensor)


def cross(every, new):
    size, rows = every[0].shape[0], new[0].shape[0]
    full = dot(jnp.concatenate(every, axis=0), jnp.concatenate(new, axis=0), NT)
    return full[:size, :rows] + (full[:size, rows:] + full[size:, :rows] + full[size:, rows:])


def joined(refs):
    return [jnp.concatenate([ref[...] for ref in refs[s::2]], axis=0) for s in range(2)]


def low_core():
    return lax.axis_index("cols") % 2 == 0


def shares(value):
    half = value.shape[0] // 2
    low, high = value[:half], value[half:]
    return jnp.where(low_core(), low, high), jnp.where(low_core(), high, low)


def merged(mine, other):
    return jnp.concatenate([jnp.where(low_core(), mine, other), jnp.where(low_core(), other, mine)], axis=0)


def in_turn(ref, shifts):
    me = lax.axis_index("fibre")
    return jnp.concatenate([ref[me ^ shift] for shift in shifts], axis=1)


def by_fibre(ref):
    return jnp.concatenate([ref[f] for f in range(ref.shape[0])], axis=1)


def put(value, shifts, ref):
    me, rows = lax.axis_index("fibre"), ref.shape[2]
    for p, shift in enumerate(shifts):
        ref[me ^ shift] = value[:, p * rows : (p + 1) * rows]


def arrive_kernel(parts, before, share, *refs):
    piece = jnp.concatenate([ref[...] for ref in refs[:parts]], axis=0)
    old = refs[parts : parts + 2 * before]
    state = refs[parts + 2 * before : parts + 2 * before + bool(before)]
    high_ref, low_ref, *gram_refs = refs[parts + 2 * before + bool(before) :]
    new = halves(piece)
    high_ref[...], low_ref[...] = new
    if before:
        column = cross([jnp.concatenate(pair, axis=0) for pair in zip(joined(old), new)], new)
        side = state[0].shape[0]
        gram = jnp.concatenate([jnp.concatenate([state[0][...], column[:side].T], axis=0), column], axis=1)
    else:
        gram = cross(new, new)
    for ref, value in zip(gram_refs, shares(gram) if share else [gram]):
        ref[...] = value


def arrive(parts, old, state, share):
    rows, width = sum(part.shape[0] for part in parts), parts[0].shape[1]
    size = sum(piece.shape[0] for piece in old[::2]) + rows
    out = (bf16(rows, width),) * 2 + ((f32(size // 2, size),) * 2 if share else (f32(size, size),))
    return pl.pallas_call(
        functools.partial(arrive_kernel, len(parts), len(old) // 2, share),
        out_shape=out,
        in_specs=[VMEM] * (len(parts) + len(old) + len(state)),
        out_specs=(VMEM,) * len(out),
        compiler_params=params(24),
        cost_estimate=pl.CostEstimate(
            flops=8 * rows * width * size, bytes_accessed=4 * width * size, transcendentals=0
        ),
        name="arrive",
    )(*parts, *old, *state)


def stripe_kernel(piece_ref, *refs):
    old, (high_ref, low_ref, mine_ref, other_ref) = refs[:-4], refs[-4:]
    new = halves(piece_ref[...])
    high_ref[...], low_ref[...] = new
    column = cross([jnp.concatenate(pair, axis=0) for pair in zip(joined(old), new)], new)
    mine_ref[...], other_ref[...] = shares(column.T)


def stripe(part, old):
    rows, width = part.shape
    size = sum(piece.shape[0] for piece in old[::2]) + rows
    return pl.pallas_call(
        stripe_kernel,
        out_shape=(bf16(rows, width),) * 2 + (f32(rows // 2, size),) * 2,
        in_specs=[VMEM] * (1 + len(old)),
        out_specs=(VMEM,) * 4,
        compiler_params=params(24),
        cost_estimate=pl.CostEstimate(
            flops=8 * rows * width * size, bytes_accessed=4 * width * size, transcendentals=0
        ),
        name="stripe",
    )(part, *old)


def late_kernel(shifts, piece_ref, basis_ref, *refs):
    old, (high_ref, low_ref, mine_ref, other_ref, to_mine_ref, to_other_ref) = refs[:-6], refs[-6:]
    new = halves(piece_ref[...])
    high_ref[...], low_ref[...] = new
    lower = cross([jnp.concatenate(pair, axis=0) for pair in zip(joined(old), new)], new).T
    mine_ref[...], other_ref[...] = shares(lower)
    side = lower.shape[1] - lower.shape[0]
    basis, split = halves(in_turn(basis_ref, shifts)), halves(lower)
    early = dot3([v[:, side:] for v in basis], [v[:, :side] for v in split], NN)
    for ref, value in zip(
        (to_mine_ref, to_other_ref), shares(jnp.concatenate([early, dot3(basis, split, NT)], axis=1))
    ):
        put(value, shifts, ref)


def late(shifts, part, basis, old):
    rows, width = part.shape
    size = sum(piece.shape[0] for piece in old[::2]) + rows
    fibres, ranks, modes = basis.shape
    return pl.pallas_call(
        functools.partial(late_kernel, shifts),
        out_shape=(bf16(rows, width),) * 2 + (f32(rows // 2, size),) * 2 + (f32(fibres, ranks // 2, modes),) * 2,
        in_specs=[VMEM] * (2 + len(old)),
        out_specs=(VMEM,) * 6,
        compiler_params=params(24),
        cost_estimate=pl.CostEstimate(
            flops=8 * rows * width * size, bytes_accessed=4 * width * size, transcendentals=0
        ),
        name="late",
    )(part, basis, *old)


def ranks_here(basis):
    half = basis.shape[0] // 2
    return jnp.where(low_core(), basis[:half], basis[half:])


def assemble_kernel(shifts, basis_ref, gram_mine, gram_other, mine_ref, other_ref, high_ref, low_ref, image_ref):
    block = merged(gram_mine[...], gram_other[...])
    lower = merged(mine_ref[...], other_ref[...])
    side = block.shape[0]
    gram = jnp.concatenate(
        [jnp.concatenate([block, lower[:, :side]], axis=0), lower.T], axis=1
    )
    split = halves(gram)
    high_ref[...], low_ref[...] = split
    basis = halves(ranks_here(in_turn(basis_ref, shifts))[:, : gram.shape[0]])
    image = dot3(basis, split, NN)
    rest = basis_ref.shape[0] * basis_ref.shape[2] - gram.shape[0]
    put(jnp.concatenate([image, jnp.zeros((image.shape[0], rest), jnp.float32)], axis=1), shifts, image_ref)


def assemble(shifts, basis, block, lower):
    size = lower[0].shape[1]
    return pl.pallas_call(
        functools.partial(assemble_kernel, shifts),
        out_shape=(bf16(size, size), bf16(size, size), f32(basis.shape[0], basis.shape[1] // 2, basis.shape[2])),
        in_specs=[VMEM] * 5,
        out_specs=(VMEM,) * 3,
        compiler_params=params(16),
        name="assemble",
    )(basis, *block, *lower)


def with_stripe(early, image, stripe):
    side = stripe[0].shape[1] - stripe[0].shape[0]
    late = dot3(image, stripe, NT)
    early = early + dot3([v[:, side:] for v in image], [v[:, :side] for v in stripe], NN)
    return jnp.concatenate([early, late], axis=1)


def second_kernel(shifts, image_ref, high_ref, low_ref, mine_ref, other_ref, out_ref):
    image = halves(in_turn(image_ref, shifts))
    side = high_ref.shape[0]
    early = dot3([v[:, :side] for v in image], (high_ref[...], low_ref[...]), NN)
    put(with_stripe(early, image, halves(merged(mine_ref[...], other_ref[...]))), shifts, out_ref)


def second(shifts, image, gram, stripe):
    return pl.pallas_call(
        functools.partial(second_kernel, shifts),
        out_shape=f32(*image.shape),
        in_specs=[VMEM] * 5,
        out_specs=VMEM,
        compiler_params=params(16),
        name="second",
    )(image, *gram, *stripe)


def factor_kernel(mine_ref, other_ref, out_ref):
    image = merged(by_fibre(mine_ref), by_fibre(other_ref))
    out_ref[...] = inverse_factor(dot(image, image, NT, HIGHEST))


def factor(mine, other):
    ranks = 2 * mine.shape[1]
    return pl.pallas_call(
        factor_kernel,
        out_shape=f32(ranks, ranks),
        in_specs=[VMEM] * 2,
        out_specs=VMEM,
        compiler_params=params(8),
        cost_estimate=pl.CostEstimate(flops=40 * ranks**3, bytes_accessed=8 * mine.size, transcendentals=0),
        name="factor",
    )(mine, other)


def close_kernel(shifts, mine_ref, other_ref, inverse_ref, *refs):
    pieces, (core_ref, basis_ref, slab, basis_slab, sems) = refs[:-5], refs[-5:]
    first = inverse_ref[...]
    image = dot(first, merged(by_fibre(mine_ref), by_fibre(other_ref)), NN, HIGHEST)
    turned = dot(first, merged(in_turn(mine_ref, shifts), in_turn(other_ref, shifts)), NN, HIGHEST)
    parts = halves(turned)
    width = slab.shape[1]
    chunk = min(PROJECT, width)
    raw = {}

    def project(c):
        columns = [jnp.concatenate([ref[:, c : c + chunk] for ref in pieces[k::2]], axis=0) for k in range(2)]
        raw[c] = dot3(parts, columns, NN)

    steps = [functools.partial(project, c) for c in range(0, width, chunk)]
    inverse = inverse_factor(dot(image, image, NT, HIGHEST), steps)
    basis_slab[...] = dot(inverse, image, NN, HIGHEST)
    stores = [pltpu.make_async_copy(basis_slab, basis_ref, sems.at[0])]
    stores[0].start()
    split = halves(inverse)
    for n, c in enumerate(range(0, width, chunk)):
        slab[:, c : c + chunk] = dot3(split, halves(raw[c]), NN)
        stores.append(
            pltpu.make_async_copy(slab.at[:, pl.ds(c, chunk)], core_ref.at[:, 0, 0, pl.ds(c, chunk)], sems.at[n + 1])
        )
        stores[-1].start()
    for store in stores:
        store.wait()


def close(shifts, mine, other, inverse, pieces):
    fibres, half, rows = mine.shape
    width = pieces[0].shape[1]
    return pl.pallas_call(
        functools.partial(close_kernel, shifts),
        out_shape=(f32(2 * half, 1, 1, width), f32(2 * half, fibres * rows)),
        in_specs=[VMEM] * (3 + len(pieces)),
        out_specs=(ANY, ANY),
        scratch_shapes=[
            pltpu.VMEM((2 * half, width), jnp.float32),
            pltpu.VMEM((2 * half, fibres * rows), jnp.float32),
            pltpu.SemaphoreType.DMA((width // min(PROJECT, width) + 1,)),
        ],
        compiler_params=params(24),
        name="close",
    )(mine, other, inverse, *pieces)


def swap(value, axis, size, bit):
    return lax.ppermute(value, axis, [(i, i ^ bit) for i in range(size)])


def bits(size):
    return [1 << b for b in range(size.bit_length() - 1)]


def crossings(flips):
    return [flips[i : i + 2] for i in range(0, len(flips), 2)]


def over_chips(value, axis, size):
    for flips in crossings(bits(size)[axis == "cols" :]):
        if len(flips) == 1:
            value = value + swap(value, axis, size, flips[0])
            continue
        one, two, three = (swap(value, axis, size, flip) for flip in (*flips, flips[0] ^ flips[1]))
        value = (value + one) + (two + three)
    return value


def over_cols(mine, other, n_cols):
    mine = over_chips(mine + swap(other, "cols", n_cols, 1), "cols", n_cols)
    return mine, swap(mine, "cols", n_cols, 1)


def turns(n_fibre):
    images = [n_fibre - 1] + bits(n_fibre)[:-1]
    out = []
    for p in range(n_fibre):
        shift = 0
        for b, image in enumerate(images):
            shift ^= image if p >> b & 1 else 0
        out.append(shift)
    return out


def shards(n_fibre, n_cols, tensor, initial):
    rows = tensor.shape[0]
    shifts = turns(n_fibre)
    start = initial.reshape(n_fibre, rows, initial.shape[1]).transpose(0, 2, 1)

    last = n_fibre - 1
    cuts = {1: (0, rows // 2, rows), last: (0, rows // 2, rows)}
    parts, sends = {}, 0
    for p in [*range(1, last), 0, last]:
        parts[p] = []
        for row, end in itertools.pairwise(cuts.get(p, (0, rows))):
            part = extract(shifts[p], tensor, row, end - row)
            if p:
                part = swap(part, "fibre", n_fibre, shifts[p])
                sends += 1
            parts[p].append(part)

    pieces, state = (), ()
    for p in range(last):
        high, low, *state = arrive(parts[p], pieces, state, p == last - 1)
        pieces += (high, low)
    block = over_cols(*state, n_cols)
    high, low, *lower = stripe(parts[last][0], pieces)
    pieces += (high, low)
    lower = over_cols(*lower, n_cols)
    *gram, image = assemble(shifts, start, block, lower)
    high, low, *lower, mine, other = late(shifts, parts[last][1], start, pieces)
    pieces += (high, low)
    mine = over_chips(mine + swap(other, "cols", n_cols, 1), "cols", n_cols)
    lower = over_cols(*lower, n_cols)
    mine = over_chips(mine + image, "fibre", n_fibre)
    other = swap(mine, "cols", n_cols, 1)
    inverse = factor(mine, other)
    mine = second(shifts, mine, gram, lower)
    mine = over_chips(mine, "fibre", n_fibre)
    core_slab, basis_t = close(shifts, mine, swap(mine, "cols", n_cols, 1), inverse, pieces)
    return (core_slab, basis_t.T)


def solution(mesh):
    n_fibre, n_cols = mesh.shape["fibre"], mesh.shape["cols"]
    placed = (P("fibre", "cols", None, None), P())

    def body(tensor, initial):
        return shards(n_fibre, n_cols, tensor, initial)

    return jax.shard_map(
        body,
        mesh=mesh,
        in_specs=placed,
        out_specs=(P(None, "cols", "fibre", None), P()),
        check_vma=False,
    )
```

```python
import functools
import itertools

import jax
import jax.numpy as jnp
from jax import lax
from jax.experimental import pallas as pl
from jax.experimental.pallas import tpu as pltpu
from jax.sharding import PartitionSpec as P


HIGHEST = lax.Precision.HIGHEST
VMEM = pl.BlockSpec(memory_space=pltpu.VMEM)
ANY = pl.BlockSpec(memory_space=pl.ANY)
ELIMINATE = 16
PROJECT = 512


def params(mib):
    return pltpu.CompilerParams(vmem_limit_bytes=mib << 20)


def f32(*shape):
    return jax.ShapeDtypeStruct(shape, jnp.float32)


def bf16(*shape):
    return jax.ShapeDtypeStruct(shape, jnp.bfloat16)


def dot(a, b, contract, precision=None):
    return lax.dot_general(
        a, b, (contract, ((), ())), precision=precision, preferred_element_type=jnp.float32
    )


NN = ((1,), (0,))
NT = ((1,), (1,))


def halves(value):
    high = value.astype(jnp.bfloat16)
    return high, (value - high.astype(jnp.float32)).astype(jnp.bfloat16)


def dot3(a, b, contract):
    return dot(a[0], b[0], contract) + (dot(a[0], b[1], contract) + dot(a[1], b[0], contract))


def eye(n):
    return jnp.where(
        lax.broadcasted_iota(jnp.int32, (n, n), 0) == lax.broadcasted_iota(jnp.int32, (n, n), 1), 1.0, 0.0
    ).astype(jnp.float32)


def inverse_factor(squares, beside=()):
    n = squares.shape[0]
    wide = 2 * n
    step = ELIMINATE
    start = jnp.concatenate([squares, eye(n)], axis=1)
    rows = [start[i : i + step] for i in range(0, n, step)]
    below = lax.broadcasted_iota(jnp.int32, (step, wide), 0)
    beside = list(beside)
    for t in range(n // step):
        if beside:
            beside.pop(0)()
        columns = [
            {i: jnp.broadcast_to(rows[i][:, t * step + j : t * step + j + 1], (step, wide)) for i in range(t, n // step)}
            for j in range(step)
        ]
        pivots = [rows[t][j : j + 1, :] for j in range(step)]
        update = {}
        for j in range(step):
            inverse = 1.0 / columns[j][t][j : j + 1, :]
            scaled = {i: columns[j][i] * inverse for i in range(t, n // step)}
            scaled[t] = jnp.where(below > j, scaled[t], 0.0)
            for i in range(t, n // step):
                term = scaled[i] * pivots[j]
                update[i] = update[i] + term if i in update else term
            for m in range(j + 1, step):
                pivots[m] = pivots[m] - scaled[t][m : m + 1, :] * pivots[j]
                across = columns[m][t][j : j + 1, :]
                for i in range(t, n // step):
                    columns[m][i] = columns[m][i] - scaled[i] * across
        for i in range(t, n // step):
            rows[i] = rows[i] - update[i]
    for call in beside:
        call()
    done = jnp.concatenate(rows, axis=0)
    left, right = done[:, :n], done[:, n:]
    diagonal = jnp.sum(left * eye(n), axis=1, keepdims=True)
    return right * lax.rsqrt(diagonal)


def extract_kernel(shift, row, tensor_ref, out_ref, sem):
    rows = out_ref.shape[0]
    which = lax.axis_index("fibre") ^ shift
    copy = pltpu.make_async_copy(tensor_ref.at[pl.ds(row, rows), 0, which, :], out_ref, sem)
    copy.start()
    copy.wait()


def extract(shift, tensor, row, rows):
    width = tensor.shape[3]
    return pl.pallas_call(
        functools.partial(extract_kernel, shift, row),
        out_shape=f32(rows, width),
        in_specs=[ANY],
        out_specs=VMEM,
        scratch_shapes=[pltpu.SemaphoreType.DMA(())],
        compiler_params=params(62),
        cost_estimate=pl.CostEstimate(flops=0, bytes_accessed=8 * rows * width, transcendentals=0),
        name="extract",
    )(tensor)


def cross(every, new):
    size, rows = every[0].shape[0], new[0].shape[0]
    full = dot(jnp.concatenate(every, axis=0), jnp.concatenate(new, axis=0), NT)
    return full[:size, :rows] + (full[:size, rows:] + full[size:, :rows] + full[size:, rows:])


def joined(refs):
    return [jnp.concatenate([ref[...] for ref in refs[s::2]], axis=0) for s in range(2)]


def low_core():
    return lax.axis_index("cols") % 2 == 0


def shares(value):
    half = value.shape[0] // 2
    low, high = value[:half], value[half:]
    return jnp.where(low_core(), low, high), jnp.where(low_core(), high, low)


def merged(mine, other):
    return jnp.concatenate([jnp.where(low_core(), mine, other), jnp.where(low_core(), other, mine)], axis=0)


def near():
    return lax.axis_index("cols") // 2 % 2 == 0


def ordered(first, mine, other):
    return jnp.concatenate([jnp.where(first, mine, other), jnp.where(first, other, mine)], axis=0)


def quarters(refs, read):
    mine, core, chip, both = (read(ref) for ref in refs)
    return ordered(low_core(), ordered(near(), mine, chip), ordered(near(), core, both))


def in_turn(ref, shifts):
    me = lax.axis_index("fibre")
    return jnp.concatenate([ref[me ^ shift] for shift in shifts], axis=1)


def by_fibre(ref):
    return jnp.concatenate([ref[f] for f in range(ref.shape[0])], axis=1)


def put(value, shifts, ref):
    me, rows = lax.axis_index("fibre"), ref.shape[2]
    for p, shift in enumerate(shifts):
        ref[me ^ shift] = value[:, p * rows : (p + 1) * rows]


def arrive_kernel(parts, before, share, *refs):
    piece = jnp.concatenate([ref[...] for ref in refs[:parts]], axis=0)
    old = refs[parts : parts + 2 * before]
    state = refs[parts + 2 * before : parts + 2 * before + bool(before)]
    high_ref, low_ref, *gram_refs = refs[parts + 2 * before + bool(before) :]
    new = halves(piece)
    high_ref[...], low_ref[...] = new
    if before:
        column = cross([jnp.concatenate(pair, axis=0) for pair in zip(joined(old), new)], new)
        side = state[0].shape[0]
        gram = jnp.concatenate([jnp.concatenate([state[0][...], column[:side].T], axis=0), column], axis=1)
    else:
        gram = cross(new, new)
    for ref, value in zip(gram_refs, shares(gram) if share else [gram]):
        ref[...] = value


def arrive(parts, old, state, share):
    rows, width = sum(part.shape[0] for part in parts), parts[0].shape[1]
    size = sum(piece.shape[0] for piece in old[::2]) + rows
    out = (bf16(rows, width),) * 2 + ((f32(size // 2, size),) * 2 if share else (f32(size, size),))
    return pl.pallas_call(
        functools.partial(arrive_kernel, len(parts), len(old) // 2, share),
        out_shape=out,
        in_specs=[VMEM] * (len(parts) + len(old) + len(state)),
        out_specs=(VMEM,) * len(out),
        compiler_params=params(24),
        cost_estimate=pl.CostEstimate(
            flops=8 * rows * width * size, bytes_accessed=4 * width * size, transcendentals=0
        ),
        name="arrive",
    )(*parts, *old, *state)


def stripe_kernel(piece_ref, *refs):
    old, (high_ref, low_ref, mine_ref, other_ref) = refs[:-4], refs[-4:]
    new = halves(piece_ref[...])
    high_ref[...], low_ref[...] = new
    column = cross([jnp.concatenate(pair, axis=0) for pair in zip(joined(old), new)], new)
    mine_ref[...], other_ref[...] = shares(column.T)


def stripe(part, old):
    rows, width = part.shape
    size = sum(piece.shape[0] for piece in old[::2]) + rows
    return pl.pallas_call(
        stripe_kernel,
        out_shape=(bf16(rows, width),) * 2 + (f32(rows // 2, size),) * 2,
        in_specs=[VMEM] * (1 + len(old)),
        out_specs=(VMEM,) * 4,
        compiler_params=params(24),
        cost_estimate=pl.CostEstimate(
            flops=8 * rows * width * size, bytes_accessed=4 * width * size, transcendentals=0
        ),
        name="stripe",
    )(part, *old)


def late_kernel(shifts, piece_ref, basis_ref, *refs):
    old, (high_ref, low_ref, mine_ref, other_ref, to_mine_ref, to_other_ref) = refs[:-6], refs[-6:]
    new = halves(piece_ref[...])
    high_ref[...], low_ref[...] = new
    lower = cross([jnp.concatenate(pair, axis=0) for pair in zip(joined(old), new)], new).T
    mine_ref[...], other_ref[...] = shares(lower)
    side = lower.shape[1] - lower.shape[0]
    basis, split = halves(in_turn(basis_ref, shifts)), halves(lower)
    early = dot3([v[:, side:] for v in basis], [v[:, :side] for v in split], NN)
    for ref, value in zip(
        (to_mine_ref, to_other_ref), shares(jnp.concatenate([early, dot3(basis, split, NT)], axis=1))
    ):
        half = value.shape[0] // 2
        put(ordered(near(), value[:half], value[half:]), shifts, ref)


def late(shifts, part, basis, old):
    rows, width = part.shape
    size = sum(piece.shape[0] for piece in old[::2]) + rows
    fibres, ranks, modes = basis.shape
    return pl.pallas_call(
        functools.partial(late_kernel, shifts),
        out_shape=(bf16(rows, width),) * 2 + (f32(rows // 2, size),) * 2 + (f32(fibres, ranks // 2, modes),) * 2,
        in_specs=[VMEM] * (2 + len(old)),
        out_specs=(VMEM,) * 6,
        compiler_params=params(24),
        cost_estimate=pl.CostEstimate(
            flops=8 * rows * width * size, bytes_accessed=4 * width * size, transcendentals=0
        ),
        name="late",
    )(part, basis, *old)


def ranks_here(basis):
    mine, _ = shares(basis)
    half = mine.shape[0] // 2
    return jnp.where(near(), mine[:half], mine[half:])


def assemble_kernel(shifts, basis_ref, gram_mine, gram_other, mine_ref, other_ref, high_ref, low_ref, image_ref):
    block = merged(gram_mine[...], gram_other[...])
    lower = merged(mine_ref[...], other_ref[...])
    side = block.shape[0]
    gram = jnp.concatenate(
        [jnp.concatenate([block, lower[:, :side]], axis=0), lower.T], axis=1
    )
    split = halves(gram)
    high_ref[...], low_ref[...] = split
    basis = halves(ranks_here(in_turn(basis_ref, shifts))[:, : gram.shape[0]])
    image = dot3(basis, split, NN)
    rest = basis_ref.shape[0] * basis_ref.shape[2] - gram.shape[0]
    put(jnp.concatenate([image, jnp.zeros((image.shape[0], rest), jnp.float32)], axis=1), shifts, image_ref)


def assemble(shifts, basis, block, lower):
    size = lower[0].shape[1]
    return pl.pallas_call(
        functools.partial(assemble_kernel, shifts),
        out_shape=(bf16(size, size), bf16(size, size), f32(basis.shape[0], basis.shape[1] // 4, basis.shape[2])),
        in_specs=[VMEM] * 5,
        out_specs=(VMEM,) * 3,
        compiler_params=params(16),
        name="assemble",
    )(basis, *block, *lower)


def with_stripe(early, image, stripe):
    side = stripe[0].shape[1] - stripe[0].shape[0]
    late = dot3(image, stripe, NT)
    early = early + dot3([v[:, side:] for v in image], [v[:, :side] for v in stripe], NN)
    return jnp.concatenate([early, late], axis=1)


def second_kernel(shifts, image_ref, high_ref, low_ref, mine_ref, other_ref, out_ref):
    image = halves(in_turn(image_ref, shifts))
    side = high_ref.shape[0]
    early = dot3([v[:, :side] for v in image], (high_ref[...], low_ref[...]), NN)
    put(with_stripe(early, image, halves(merged(mine_ref[...], other_ref[...]))), shifts, out_ref)


def second(shifts, image, gram, stripe):
    return pl.pallas_call(
        functools.partial(second_kernel, shifts),
        out_shape=f32(*image.shape),
        in_specs=[VMEM] * 5,
        out_specs=VMEM,
        compiler_params=params(16),
        name="second",
    )(image, *gram, *stripe)


def factor_kernel(*refs):
    image = quarters(refs[:-1], by_fibre)
    refs[-1][...] = inverse_factor(dot(image, image, NT, HIGHEST))


def factor(*shares):
    ranks = 4 * shares[0].shape[1]
    return pl.pallas_call(
        factor_kernel,
        out_shape=f32(ranks, ranks),
        in_specs=[VMEM] * 4,
        out_specs=VMEM,
        compiler_params=params(8),
        cost_estimate=pl.CostEstimate(flops=40 * ranks**3, bytes_accessed=16 * shares[0].size, transcendentals=0),
        name="factor",
    )(*shares)


def close_kernel(shifts, inverse_ref, *refs):
    share_refs, refs = refs[:4], refs[4:]
    pieces, (core_ref, basis_ref, slab, basis_slab, sems) = refs[:-5], refs[-5:]
    first = inverse_ref[...]
    image = dot(first, quarters(share_refs, by_fibre), NN, HIGHEST)
    turned = dot(first, quarters(share_refs, lambda ref: in_turn(ref, shifts)), NN, HIGHEST)
    parts = halves(turned)
    width = slab.shape[1]
    chunk = min(PROJECT, width)
    raw = {}

    def project(c):
        columns = [jnp.concatenate([ref[:, c : c + chunk] for ref in pieces[k::2]], axis=0) for k in range(2)]
        raw[c] = dot3(parts, columns, NN)

    steps = [functools.partial(project, c) for c in range(0, width, chunk)]
    inverse = inverse_factor(dot(image, image, NT, HIGHEST), steps)
    basis_slab[...] = dot(inverse, image, NN, HIGHEST)
    stores = [pltpu.make_async_copy(basis_slab, basis_ref, sems.at[0])]
    stores[0].start()
    split = halves(inverse)
    for n, c in enumerate(range(0, width, chunk)):
        slab[:, c : c + chunk] = dot3(split, halves(raw[c]), NN)
        stores.append(
            pltpu.make_async_copy(slab.at[:, pl.ds(c, chunk)], core_ref.at[:, 0, 0, pl.ds(c, chunk)], sems.at[n + 1])
        )
        stores[-1].start()
    for store in stores:
        store.wait()


def close(shifts, shares, inverse, pieces):
    fibres, quarter, rows = shares[0].shape
    ranks = 4 * quarter
    width = pieces[0].shape[1]
    return pl.pallas_call(
        functools.partial(close_kernel, shifts),
        out_shape=(f32(ranks, 1, 1, width), f32(ranks, fibres * rows)),
        in_specs=[VMEM] * (5 + len(pieces)),
        out_specs=(ANY, ANY),
        scratch_shapes=[
            pltpu.VMEM((ranks, width), jnp.float32),
            pltpu.VMEM((ranks, fibres * rows), jnp.float32),
            pltpu.SemaphoreType.DMA((width // min(PROJECT, width) + 1,)),
        ],
        compiler_params=params(24),
        name="close",
    )(inverse, *shares, *pieces)


def swap(value, axis, size, bit):
    return lax.ppermute(value, axis, [(i, i ^ bit) for i in range(size)])


def bits(size):
    return [1 << b for b in range(size.bit_length() - 1)]


def crossings(flips):
    return [flips[i : i + 2] for i in range(0, len(flips), 2)]


def over_flips(value, axis, size, flips):
    if len(flips) == 1:
        return value + swap(value, axis, size, flips[0])
    one, two, three = (swap(value, axis, size, flip) for flip in (*flips, flips[0] ^ flips[1]))
    return (value + one) + (two + three)


def over_chips(value, axis, size):
    for flips in crossings(bits(size)[axis == "cols" :]):
        value = over_flips(value, axis, size, flips)
    return value


def over_cols(mine, other, n_cols):
    mine = over_chips(mine + swap(other, "cols", n_cols, 1), "cols", n_cols)
    return mine, swap(mine, "cols", n_cols, 1)


def to_quarters(mine, other, n_cols):
    mine = mine + swap(other, "cols", n_cols, 1)
    half = mine.shape[1] // 2
    here, there = mine[:, :half], mine[:, half:]
    (chip, side), *rest = crossings(bits(n_cols)[1:])
    one = swap(here, "cols", n_cols, side)
    two, three = swap(there, "cols", n_cols, chip), swap(there, "cols", n_cols, chip ^ side)
    here = (here + one) + (two + three)
    for one_more in rest:
        here = over_flips(here, "cols", n_cols, one_more)
    return here


def from_quarters(mine, n_cols):
    return mine, *(swap(mine, "cols", n_cols, flip) for flip in (1, 2, 3))


def turns(n_fibre):
    images = [n_fibre - 1] + bits(n_fibre)[:-1]
    out = []
    for p in range(n_fibre):
        shift = 0
        for b, image in enumerate(images):
            shift ^= image if p >> b & 1 else 0
        out.append(shift)
    return out


def shards(n_fibre, n_cols, tensor, initial):
    rows = tensor.shape[0]
    shifts = turns(n_fibre)
    start = initial.reshape(n_fibre, rows, initial.shape[1]).transpose(0, 2, 1)

    last = n_fibre - 1
    cuts = {1: (0, rows // 2, rows), last: (0, rows // 2, rows)}
    parts, sends = {}, 0
    for p in [*range(1, last), 0, last]:
        parts[p] = []
        for row, end in itertools.pairwise(cuts.get(p, (0, rows))):
            part = extract(shifts[p], tensor, row, end - row)
            if p:
                part = swap(part, "fibre", n_fibre, shifts[p])
                sends += 1
            parts[p].append(part)

    pieces, state = (), ()
    for p in range(last):
        high, low, *state = arrive(parts[p], pieces, state, p == last - 1)
        pieces += (high, low)
    block = over_cols(*state, n_cols)
    high, low, *lower = stripe(parts[last][0], pieces)
    pieces += (high, low)
    lower = over_cols(*lower, n_cols)
    *gram, image = assemble(shifts, start, block, lower)
    high, low, *lower, mine, other = late(shifts, parts[last][1], start, pieces)
    pieces += (high, low)
    mine = to_quarters(mine, other, n_cols)
    lower = over_cols(*lower, n_cols)
    mine = over_chips(mine + image, "fibre", n_fibre)
    shares_1 = from_quarters(mine, n_cols)
    inverse = factor(*shares_1)
    mine = second(shifts, mine, gram, lower)
    mine = over_chips(mine, "fibre", n_fibre)
    shares_2 = from_quarters(mine, n_cols)
    core_slab, basis_t = close(shifts, shares_2, inverse, pieces)
    return (core_slab, basis_t.T)


def solution(mesh):
    n_fibre, n_cols = mesh.shape["fibre"], mesh.shape["cols"]
    placed = (P("fibre", "cols", None, None), P())

    def body(tensor, initial):
        return shards(n_fibre, n_cols, tensor, initial)

    return jax.shard_map(
        body,
        mesh=mesh,
        in_specs=placed,
        out_specs=(P(None, "cols", "fibre", None), P()),
        check_vma=False,
    )
```
